32 devices in a mesh: grp: 2 (over x), occ: 16 (over z, y, core).
Axes of the slice: x: 2, y: 2, z: 4, core: 2. Of those that a mesh axis runs over, the one named last changes fastest.
Arguments:
- orbital_blocks: bfloat16 [32, 512, 4096], P(('grp', 'occ')), parts along dimension 0, may hold values from -0.75 to 0.75
- eps_occ: float32 [32], P('grp'), parts along dimension 0, may hold values from -2 to -0.5
- eps_vir: float32 [1024], P('grp'), parts along dimension 0, may hold values from 0.2 to 3
- pair_mask: int32 [32, 2], P('grp'), parts along dimension 0, may hold values 0 or 1
Outputs:
- grad_density: float32 [32, 512, 4096], P(('grp', 'occ')), parts along dimension 0
The draws below stay inside these ranges and needn't reach their ends.
There are 2 independent parts, one for each index of `grp`. The reference program is written for one: setup_inputs(seed, part) draws one part's arguments, and reference() takes and returns one part's arrays. A program takes and returns all parts, laid end to end along the dimension named above; each array names one. Nothing has to cross between parts.
Inputs may be any that keep to these rules, and one draw needn't show every extreme that they name: pair_mask[i, 0] selects the pair (i, i + 1) and pair_mask[i, 1] the pair (i, i + 8); entries of pairs that do not exist are unused.
All inputs are finite; a program needn't handle non-finite values.
Results may differ from the reference program's by a relative error of at most 0.0026.
Values may be sent and summed in bfloat16 or wider, within the bound.
A program may use at most 128 MiB of HBM per device.

```python
import jax
import jax.numpy as jnp
from jax import lax

NVIR = 512
NAUX = 4096
NOCC = 16
N_OCC = 16


def with_ends(drawn, own_key, low, top_value):
    longest = drawn.shape.index(max(drawn.shape))
    spots = []
    for shift in (0, 1):
        where = [jax.random.randint(jax.random.fold_in(own_key, axis), (), 0, length) for axis, length in enumerate(drawn.shape)]
        where[longest] = (where[longest] + shift) % drawn.shape[longest]
        spots.append(tuple(where))
    return drawn.at[spots[0]].set(low).at[spots[1]].set(top_value)


def shard_levels(stream_key, shape, shards, least, largest):
    gain, own = 1.0, jax.random.fold_in(stream_key, 6)
    for position, shards_of in shards:
        heights = jnp.exp(jax.random.uniform(jax.random.fold_in(own, position), (shards_of,), jnp.float32, least / len(shards), largest / len(shards)))
        gain = gain * jnp.repeat(heights, shape[position] // shards_of).reshape([-1 if axis == position else 1 for axis in range(len(shape))])
    return gain


def scatter_about(key, extent, deviation, reach, shards=(), held_as=jnp.bfloat16):
    loudness = shard_levels(key, extent, shards, -0.22, 0.18) if shards else 1.0
    array = jax.random.normal(key, extent, jnp.float32) * deviation * loudness
    return jnp.minimum(jnp.maximum(array, -reach), reach).astype(held_as)


def setup_inputs(seed: int = 0, part: int = 0) -> dict:
    arg_keys = jax.random.split(jax.random.key(seed), 5)
    part_keys = jax.random.split(jax.random.fold_in(arg_keys[4], part), 5)
    orbital_blocks = scatter_about(part_keys[0], (NOCC, NVIR, NAUX), (max(8, NAUX // 64)) ** -0.5, 0.75, ((0, 16),))
    eps_occ = jnp.clip(jax.random.uniform(part_keys[1], (NOCC,), jnp.float32, -2.0, -0.5), -2.0, -0.5)
    eps_vir = jnp.clip(jax.random.uniform(part_keys[2], (NVIR,), jnp.float32, 0.2, 3.0), 0.2, 3.0)
    pair_mask = with_ends((jax.random.randint(part_keys[3], (NOCC, 2), 0, 4) < 3).astype(jnp.int32), jax.random.fold_in(part_keys[3], 1), 0, 1)
    return {"orbital_blocks": orbital_blocks, "eps_occ": eps_occ, "eps_vir": eps_vir, "pair_mask": pair_mask}


def pair_term(blocks, eps_occ, eps_vir, home, partner, keep_pair):
    integrals = jnp.dot(blocks[home], blocks[partner].T, preferred_element_type=jnp.float32)
    denominator = eps_vir[:, None] + eps_vir[None, :] - eps_occ[home] - eps_occ[partner]
    single = -integrals / denominator
    weights = jnp.where(keep_pair, 2.0 * single - single.T, 0.0).astype(jnp.bfloat16)
    return jnp.dot(weights, blocks[partner], preferred_element_type=jnp.float32)


def reference(orbital_blocks, eps_occ, eps_vir, pair_mask):
    total = orbital_blocks.shape[0]
    spacing = total // N_OCC
    half_window = total // 2

    def one_orbital(home):
        upper = jnp.minimum(home + spacing, total - 1).astype(jnp.int32)
        lower = jnp.maximum(home - spacing, 0).astype(jnp.int32)
        across = ((home + half_window) % total).astype(jnp.int32)
        keep_upper = (home + spacing < total) & (pair_mask[home, 0] == 1)
        keep_lower = (home >= spacing) & (pair_mask[lower, 0] == 1)
        across_row = jnp.where(home < half_window, home, home - half_window).astype(jnp.int32)
        keep_across = pair_mask[across_row, 1] == 1
        result = pair_term(orbital_blocks, eps_occ, eps_vir, home, upper, keep_upper)
        result = result + pair_term(orbital_blocks, eps_occ, eps_vir, home, lower, keep_lower)
        result = result + pair_term(orbital_blocks, eps_occ, eps_vir, home, across, keep_across)
        return result

    return lax.map(one_orbital, jnp.arange(total, dtype=jnp.int32))
```

```python
import functools

import jax
import jax.numpy as jnp
from jax import lax
from jax.experimental import pallas as pl
from jax.experimental.pallas import tpu as pltpu
from jax.sharding import PartitionSpec as P

MESH = pl.DeviceIdType.MESH
CHUNKS = 16
LOWER, UPPER, ACROSS = 0, 1, 2


def gather_kernel(
    count, own_hbm, eps_vir, eps_occ, mask, landed, weights,
    own, total, level, own_sem, up_sem, down_sem, far_sem, relay_sem, recv_sem,
):
    me = lax.axis_index("occ")
    half = count // 2
    width = own.shape[2]
    size = own.shape[1]
    last = count - 1
    partner = lax.rem(me + half, count)
    sends_up = (me < last) & (me != half - 1)
    sends_down = (me > 0) & (me != half)
    relays = (me == 0) | (me == last)
    late = (me == half - 1) | (me == half)
    relay_to = jnp.where(me == 0, half - 1, half)
    relay_slot = jnp.where(me == 0, UPPER, LOWER)
    relay_peer = jnp.where(me == half - 1, 0, jnp.where(me == half, last, relay_to))
    late_slot = jnp.where(me == half - 1, UPPER, LOWER)
    one = lambda flag: jnp.where(flag, 1, 0)

    def signal(to):
        pl.semaphore_signal(
            pltpu.get_barrier_semaphore(), inc=1, device_id={"occ": to}, device_id_type=MESH
        )

    signal(partner)
    pl.when(sends_up)(lambda: signal(me + 1))
    pl.when(sends_down)(lambda: signal(me - 1))
    pl.when(relays | late)(lambda: signal(relay_peer))
    pl.semaphore_wait(
        pltpu.get_barrier_semaphore(), 1 + one(sends_up) + one(sends_down) + one(relays | late)
    )

    def remote(source, k, slot, send_sem, to):
        return pltpu.make_async_remote_copy(
            src_ref=source, dst_ref=landed.at[k, slot], send_sem=send_sem.at[k],
            recv_sem=recv_sem.at[slot, k], device_id={"occ": to}, device_id_type=MESH,
        )

    def columns(k):
        return own_hbm.at[:, pl.ds(pl.multiple_of(k * width, width), width)]

    def up(k):
        return remote(columns(k), k, LOWER, up_sem, me + 1)

    def down(k):
        return remote(columns(k), k, UPPER, down_sem, me - 1)

    def far(k):
        return remote(columns(k), k, ACROSS, far_sem, partner)

    def relay(k):
        return remote(landed.at[k, ACROSS], k, relay_slot, relay_sem, relay_to)

    def loaded(k):
        return pltpu.make_async_copy(columns(k), own.at[k], own_sem.at[k])

    def received(k, slot):
        remote(landed.at[k, slot], k, slot, far_sem, partner).wait_recv()

    @pl.loop(0, CHUNKS)
    def _(k):
        pl.when(sends_up)(lambda: up(k).start())
        pl.when(sends_down)(lambda: down(k).start())

    @pl.loop(0, CHUNKS)
    def _(k):
        far(k).start()

    @pl.loop(0, CHUNKS)
    def _(k):
        loaded(k).start()

    rows = jnp.broadcast_to(eps_vir[...], (size, size))
    level[...] = rows + rows.T
    total[...] = jnp.zeros_like(total)

    @pl.when(me == 0)
    def _():
        landed[:, LOWER] = jnp.zeros((CHUNKS, size, width), landed.dtype)

    @pl.when(me == last)
    def _():
        landed[:, UPPER] = jnp.zeros((CHUNKS, size, width), landed.dtype)

    def accumulate(k, slot):
        received(k, slot)
        total[slot] += lax.dot_general(
            own[k], landed[k, slot], (((1,), (1,)), ((), ())), preferred_element_type=jnp.float32
        )

    def finish(slot):
        lower, upper = jnp.maximum(me - 1, 0), jnp.minimum(me + 1, last)
        other = (lower, upper, partner)[slot]
        bit = (mask[0, lower], mask[0, me], mask[1, jnp.minimum(me, partner)])[slot]
        real = (me > 0, me < last, me >= 0)[slot]
        keep = jnp.where(bit == 1, 1.0, 0.0) * jnp.where(real, 1.0, 0.0)
        single = -total[slot] / (level[...] - (eps_occ[me] + eps_occ[other]))
        doubled = (2.0 * single - single.T) * keep
        weights[:, slot * size : (slot + 1) * size] = doubled.astype(weights.dtype)

    lower_early = (me > 0) & (me != half)
    upper_early = (me < last) & (me != half - 1)

    @pl.loop(0, CHUNKS)
    def _(k):
        loaded(k).wait()
        pl.when(lower_early)(lambda: accumulate(k, LOWER))
        pl.when(upper_early)(lambda: accumulate(k, UPPER))

    pl.when(me != half)(lambda: finish(LOWER))
    pl.when(me != half - 1)(lambda: finish(UPPER))

    @pl.loop(0, CHUNKS)
    def _(k):
        received(k, ACROSS)
        pl.when(relays)(lambda: relay(k).start())
        total[ACROSS] += lax.dot_general(
            own[k], landed[k, ACROSS], (((1,), (1,)), ((), ())), preferred_element_type=jnp.float32
        )
        pl.when(late)(lambda: accumulate(k, late_slot))

    finish(ACROSS)
    pl.when(me == half)(lambda: finish(LOWER))
    pl.when(me == half - 1)(lambda: finish(UPPER))

    @pl.loop(0, CHUNKS)
    def _(k):
        pl.when(sends_up)(lambda: up(k).wait_send())
        pl.when(sends_down)(lambda: down(k).wait_send())
        far(k).wait_send()
        pl.when(relays)(lambda: relay(k).wait_send())


def apply_kernel(landed, weights, out, staged, sems):
    size, width = staged.shape[1:]

    def stored(k):
        slot = lax.rem(k, 2)
        at = pl.ds(pl.multiple_of(k * width, width), width)
        return pltpu.make_async_copy(staged.at[slot], out.at[:, at], sems.at[slot])

    @pl.loop(0, CHUNKS)
    def _(k):
        pl.when(k >= 2)(lambda: stored(k - 2).wait())
        blocks = landed[k].reshape(3 * size, width)
        staged[lax.rem(k, 2)] = jnp.dot(weights[...], blocks, preferred_element_type=jnp.float32)
        stored(k).start()

    stored(CHUNKS - 2).wait()
    stored(CHUNKS - 1).wait()


def local(orbital_blocks, eps_occ, eps_vir, pair_mask):
    _, size, aux = orbital_blocks.shape
    width = aux // CHUNKS
    count = lax.axis_size("occ")
    vmem = pl.BlockSpec(memory_space=pltpu.VMEM)
    smem = pl.BlockSpec(memory_space=pltpu.SMEM)
    hbm = pl.BlockSpec(memory_space=pl.ANY)
    per_chunk = pltpu.SemaphoreType.DMA((CHUNKS,))
    landed, weights = pl.pallas_call(
        functools.partial(gather_kernel, count),
        out_shape=(
            pltpu.VMEM((CHUNKS, 3, size, width), jnp.bfloat16),
            pltpu.VMEM((size, 3 * size), jnp.bfloat16),
        ),
        in_specs=[hbm, vmem, smem, smem],
        out_specs=(vmem, vmem),
        scratch_shapes=[
            pltpu.VMEM((CHUNKS, size, width), jnp.bfloat16),
            pltpu.VMEM((3, size, size), jnp.float32),
            pltpu.VMEM((size, size), jnp.float32),
            per_chunk, per_chunk, per_chunk, per_chunk, per_chunk,
            pltpu.SemaphoreType.DMA((3, CHUNKS)),
        ],
        compiler_params=pltpu.CompilerParams(
            collective_id=0, has_side_effects=True, vmem_limit_bytes=44 * 2**20
        ),
    )(orbital_blocks[0], eps_vir[None], eps_occ, pair_mask.T)
    gradient = pl.pallas_call(
        apply_kernel,
        out_shape=jax.ShapeDtypeStruct((size, aux), jnp.float32),
        in_specs=[vmem, vmem],
        out_specs=hbm,
        scratch_shapes=[
            pltpu.VMEM((2, size, width), jnp.float32),
            pltpu.SemaphoreType.DMA((2,)),
        ],
        compiler_params=pltpu.CompilerParams(vmem_limit_bytes=44 * 2**20),
    )(
        pltpu.with_memory_space_constraint(landed, pltpu.VMEM),
        pltpu.with_memory_space_constraint(weights, pltpu.VMEM),
    )
    return gradient[None]


def solution(mesh):
    in_specs = (P(("grp", "occ"), None, None), P("grp"), P("grp"), P("grp", None))
    out_specs = P(("grp", "occ"), None, None)
    return jax.shard_map(local, mesh=mesh, in_specs=in_specs, out_specs=out_specs, check_vma=False)
```

```python
import functools

import jax
import jax.numpy as jnp
from jax import lax
from jax.experimental import pallas as pl
from jax.experimental.pallas import tpu as pltpu
from jax.sharding import PartitionSpec as P

MESH = pl.DeviceIdType.MESH
CHUNKS = 16
LOWER, UPPER, ACROSS = 0, 1, 2


def gather_kernel(
    count, own_hbm, eps_vir, eps_occ, mask, across, weights, gradient,
    near, near_weights, own, total, level,
    own_sem, up_sem, down_sem, far_sem, relay_sem, near_recv, across_recv,
):
    me = lax.axis_index("occ")
    half = count // 2
    size, width = own.shape[1:]
    last = count - 1
    partner = lax.rem(me + half, count)
    sends_up = (me < last) & (me != half - 1)
    sends_down = (me > 0) & (me != half)
    relays = (me == 0) | (me == last)
    relayed = (me == half - 1) | (me == half)
    yields = (me == half + 1) | (me == half - 2)
    relay_to = jnp.where(me == 0, half - 1, half)
    relay_slot = jnp.where(me == 0, UPPER, LOWER)
    relay_peer = jnp.where(me == half - 1, 0, jnp.where(me == half, last, relay_to))
    one = lambda flag: jnp.where(flag, 1, 0)

    def signal(to):
        pl.semaphore_signal(
            pltpu.get_barrier_semaphore(), inc=1, device_id={"occ": to}, device_id_type=MESH
        )

    signal(partner)
    pl.when(sends_up)(lambda: signal(me + 1))
    pl.when(sends_down)(lambda: signal(me - 1))
    pl.when(relays | relayed)(lambda: signal(relay_peer))
    pl.semaphore_wait(
        pltpu.get_barrier_semaphore(), 1 + one(sends_up) + one(sends_down) + one(relays | relayed)
    )

    def columns(k):
        return own_hbm.at[:, pl.ds(pl.multiple_of(k * width, width), width)]

    def to_near(source, k, slot, send_sem, to):
        return pltpu.make_async_remote_copy(
            src_ref=source, dst_ref=near.at[k, slot], send_sem=send_sem.at[k],
            recv_sem=near_recv.at[slot, k], device_id={"occ": to}, device_id_type=MESH,
        )

    def up(k):
        return to_near(columns(k), k, LOWER, up_sem, me + 1)

    def down(k):
        return to_near(columns(k), k, UPPER, down_sem, me - 1)

    def relay(k):
        return to_near(across.at[k], k, relay_slot, relay_sem, relay_to)

    def far(k):
        return pltpu.make_async_remote_copy(
            src_ref=columns(k), dst_ref=across.at[k], send_sem=far_sem.at[k],
            recv_sem=across_recv.at[k], device_id={"occ": partner}, device_id_type=MESH,
        )

    def loaded(k):
        return pltpu.make_async_copy(columns(k), own.at[k], own_sem.at[k])

    def send_far():
        @pl.loop(0, CHUNKS)
        def _(k):
            far(k).start()

    @pl.loop(0, CHUNKS)
    def _(k):
        pl.when(sends_up)(lambda: up(k).start())
        pl.when(sends_down)(lambda: down(k).start())

    pl.when(jnp.logical_not(yields))(send_far)

    @pl.loop(0, CHUNKS)
    def _(k):
        loaded(k).start()

    rows = jnp.broadcast_to(eps_vir[...], (size, size))
    level[...] = rows + rows.T
    total[...] = jnp.zeros_like(total)

    @pl.when(me == 0)
    def _():
        near[:, LOWER] = jnp.zeros((CHUNKS, size, width), near.dtype)

    @pl.when(me == last)
    def _():
        near[:, UPPER] = jnp.zeros((CHUNKS, size, width), near.dtype)

    def overlap(k, block):
        return lax.dot_general(
            own[k], block, (((1,), (1,)), ((), ())), preferred_element_type=jnp.float32
        )

    def accumulate(k, slot):
        to_near(near.at[k, slot], k, slot, far_sem, partner).wait_recv()
        total[slot] += overlap(k, near[k, slot])

    def kept(bit, real):
        return jnp.where(bit == 1, 1.0, 0.0) * jnp.where(real, 1.0, 0.0)

    def finish(slot, keep, other):
        single = -total[slot] / (level[...] - (eps_occ[me] + eps_occ[other]))
        doubled = (2.0 * single - single.T) * keep
        near_weights[:, slot * size : (slot + 1) * size] = doubled.astype(near_weights.dtype)

    @pl.loop(0, CHUNKS)
    def _(k):
        loaded(k).wait()
        pl.when(me > 0)(lambda: accumulate(k, LOWER))
        pl.when(me < last)(lambda: accumulate(k, UPPER))

    pl.when(yields)(send_far)
    lower, upper = jnp.maximum(me - 1, 0), jnp.minimum(me + 1, last)
    finish(LOWER, kept(mask[0, lower], me > 0), lower)
    finish(UPPER, kept(mask[0, me], me < last), upper)
    level[...] = kept(mask[1, jnp.minimum(me, partner)], me >= 0) / (
        level[...] - (eps_occ[me] + eps_occ[partner])
    )

    @pl.loop(0, CHUNKS)
    def _(k):
        gradient[k] = jnp.dot(
            near_weights[...], near[k].reshape(2 * size, width), preferred_element_type=jnp.float32
        )

    @pl.loop(0, CHUNKS)
    def _(k):
        far(k).wait_recv()
        pl.when(relays)(lambda: relay(k).start())
        total[ACROSS] += overlap(k, across[k])

    single = -total[ACROSS] * level[...]
    weights[...] = (2.0 * single - single.T).astype(weights.dtype)

    @pl.loop(0, CHUNKS)
    def _(k):
        pl.when(sends_up)(lambda: up(k).wait_send())
        pl.when(sends_down)(lambda: down(k).wait_send())
        far(k).wait_send()
        pl.when(relays)(lambda: relay(k).wait_send())


def apply_kernel(across, weights, gradient, out, staged, sems):
    size, width = staged.shape[1:]

    def stored(k):
        slot = lax.rem(k, 2)
        at = pl.ds(pl.multiple_of(k * width, width), width)
        return pltpu.make_async_copy(staged.at[slot], out.at[:, at], sems.at[slot])

    @pl.loop(0, CHUNKS)
    def _(k):
        pl.when(k >= 2)(lambda: stored(k - 2).wait())
        staged[lax.rem(k, 2)] = gradient[k] + jnp.dot(
            weights[...], across[k], preferred_element_type=jnp.float32
        )
        stored(k).start()

    stored(CHUNKS - 2).wait()
    stored(CHUNKS - 1).wait()


def local(orbital_blocks, eps_occ, eps_vir, pair_mask):
    _, size, aux = orbital_blocks.shape
    width = aux // CHUNKS
    count = lax.axis_size("occ")
    vmem = pl.BlockSpec(memory_space=pltpu.VMEM)
    smem = pl.BlockSpec(memory_space=pltpu.SMEM)
    hbm = pl.BlockSpec(memory_space=pl.ANY)
    per_chunk = pltpu.SemaphoreType.DMA((CHUNKS,))
    arrived = pl.pallas_call(
        functools.partial(gather_kernel, count),
        out_shape=(
            pltpu.VMEM((CHUNKS, size, width), jnp.bfloat16),
            pltpu.VMEM((size, size), jnp.bfloat16),
            pltpu.VMEM((CHUNKS, size, width), jnp.float32),
        ),
        in_specs=[hbm, vmem, smem, smem],
        out_specs=(vmem, vmem, vmem),
        scratch_shapes=[
            pltpu.VMEM((CHUNKS, 2, size, width), jnp.bfloat16),
            pltpu.VMEM((size, 2 * size), jnp.bfloat16),
            pltpu.VMEM((CHUNKS, size, width), jnp.bfloat16),
            pltpu.VMEM((3, size, size), jnp.float32),
            pltpu.VMEM((size, size), jnp.float32),
            per_chunk, per_chunk, per_chunk, per_chunk, per_chunk,
            pltpu.SemaphoreType.DMA((2, CHUNKS)),
            per_chunk,
        ],
        compiler_params=pltpu.CompilerParams(
            collective_id=0, has_side_effects=True, vmem_limit_bytes=44 * 2**20
        ),
    )(orbital_blocks[0], eps_vir[None], eps_occ, pair_mask.T)
    gradient = pl.pallas_call(
        apply_kernel,
        out_shape=jax.ShapeDtypeStruct((size, aux), jnp.float32),
        in_specs=[vmem, vmem, vmem],
        out_specs=hbm,
        scratch_shapes=[
            pltpu.VMEM((2, size, width), jnp.float32),
            pltpu.SemaphoreType.DMA((2,)),
        ],
        compiler_params=pltpu.CompilerParams(vmem_limit_bytes=44 * 2**20),
    )(*(pltpu.with_memory_space_constraint(array, pltpu.VMEM) for array in arrived))
    return gradient[None]


def solution(mesh):
    in_specs = (P(("grp", "occ"), None, None), P("grp"), P("grp"), P("grp", None))
    out_specs = P(("grp", "occ"), None, None)
    return jax.shard_map(local, mesh=mesh, in_specs=in_specs, out_specs=out_specs, check_vma=False)
```

```python
import functools

import jax
import jax.numpy as jnp
from jax import lax
from jax.experimental import pallas as pl
from jax.experimental.pallas import tpu as pltpu
from jax.sharding import PartitionSpec as P

MESH = pl.DeviceIdType.MESH
CHUNKS = 8
LOWER, UPPER, ACROSS = 0, 1, 2


def gather_kernel(
    count, own_hbm, eps_vir, eps_occ, mask, across, weights, gradient,
    near, near_weights, own, total, level,
    own_sem, up_sem, down_sem, far_sem, relay_sem, near_recv, across_recv,
):
    me = lax.axis_index("occ")
    half = count // 2
    size, width = own.shape[1:]
    last = count - 1
    partner = lax.rem(me + half, count)
    sends_up = (me < last) & (me != half - 1)
    sends_down = (me > 0) & (me != half)
    relays = (me == 0) | (me == last)
    relayed = (me == half - 1) | (me == half)
    yields = (me == half + 1) | (me == half - 2)
    relay_to = jnp.where(me == 0, half - 1, half)
    relay_slot = jnp.where(me == 0, UPPER, LOWER)
    relay_peer = jnp.where(me == half - 1, 0, jnp.where(me == half, last, relay_to))
    one = lambda flag: jnp.where(flag, 1, 0)

    def signal(to):
        pl.semaphore_signal(
            pltpu.get_barrier_semaphore(), inc=1, device_id={"occ": to}, device_id_type=MESH
        )

    signal(partner)
    pl.when(sends_up)(lambda: signal(me + 1))
    pl.when(sends_down)(lambda: signal(me - 1))
    pl.when(relays | relayed)(lambda: signal(relay_peer))
    pl.semaphore_wait(
        pltpu.get_barrier_semaphore(), 1 + one(sends_up) + one(sends_down) + one(relays | relayed)
    )

    def columns(k):
        return own_hbm.at[:, pl.ds(pl.multiple_of(k * width, width), width)]

    def to_near(source, k, slot, send_sem, to):
        return pltpu.make_async_remote_copy(
            src_ref=source, dst_ref=near.at[k, slot], send_sem=send_sem.at[k],
            recv_sem=near_recv.at[slot, k], device_id={"occ": to}, device_id_type=MESH,
        )

    def up(k):
        return to_near(columns(k), k, LOWER, up_sem, me + 1)

    def down(k):
        return to_near(columns(k), k, UPPER, down_sem, me - 1)

    def relay(k):
        return to_near(across.at[k], k, relay_slot, relay_sem, relay_to)

    def far(k):
        return pltpu.make_async_remote_copy(
            src_ref=columns(k), dst_ref=across.at[k], send_sem=far_sem.at[k],
            recv_sem=across_recv.at[k], device_id={"occ": partner}, device_id_type=MESH,
        )

    def loaded(k):
        return pltpu.make_async_copy(columns(k), own.at[k], own_sem.at[k])

    def send_far(first):
        @pl.loop(first, CHUNKS)
        def _(k):
            far(k).start()

    pl.when(jnp.logical_not(yields))(lambda: far(0).start())

    @pl.loop(0, CHUNKS)
    def _(k):
        pl.when(sends_up)(lambda: up(k).start())
        pl.when(sends_down)(lambda: down(k).start())

    pl.when(jnp.logical_not(yields))(lambda: send_far(1))

    @pl.loop(0, CHUNKS)
    def _(k):
        loaded(k).start()

    rows = jnp.broadcast_to(eps_vir[...], (size, size))
    level[...] = rows + rows.T
    total[...] = jnp.zeros_like(total)

    @pl.when(me == 0)
    def _():
        near[:, LOWER] = jnp.zeros((CHUNKS, size, width), near.dtype)

    @pl.when(me == last)
    def _():
        near[:, UPPER] = jnp.zeros((CHUNKS, size, width), near.dtype)

    def overlap(k, block):
        return lax.dot_general(
            own[k], block, (((1,), (1,)), ((), ())), preferred_element_type=jnp.float32
        )

    def accumulate(k, slot):
        to_near(near.at[k, slot], k, slot, far_sem, partner).wait_recv()
        total[slot] += overlap(k, near[k, slot])

    def kept(bit, real):
        return jnp.where(bit == 1, 1.0, 0.0) * jnp.where(real, 1.0, 0.0)

    def finish(slot, keep, other):
        single = -total[slot] / (level[...] - (eps_occ[me] + eps_occ[other]))
        doubled = (2.0 * single - single.T) * keep
        near_weights[:, slot * size : (slot + 1) * size] = doubled.astype(near_weights.dtype)

    @pl.loop(0, CHUNKS)
    def _(k):
        loaded(k).wait()
        pl.when(me > 0)(lambda: accumulate(k, LOWER))
        pl.when(me < last)(lambda: accumulate(k, UPPER))

    pl.when(yields)(lambda: send_far(0))
    lower, upper = jnp.maximum(me - 1, 0), jnp.minimum(me + 1, last)
    finish(LOWER, kept(mask[0, lower], me > 0), lower)
    finish(UPPER, kept(mask[0, me], me < last), upper)
    level[...] = kept(mask[1, jnp.minimum(me, partner)], me >= 0) / (
        level[...] - (eps_occ[me] + eps_occ[partner])
    )

    @pl.loop(0, CHUNKS)
    def _(k):
        gradient[k] = jnp.dot(
            near_weights[...], near[k].reshape(2 * size, width), preferred_element_type=jnp.float32
        )

    @pl.loop(0, CHUNKS)
    def _(k):
        pl.when(sends_up)(lambda: up(k).wait_send())
        pl.when(sends_down)(lambda: down(k).wait_send())

    @pl.loop(0, CHUNKS)
    def _(k):
        far(k).wait_recv()
        pl.when(relays)(lambda: relay(k).start())
        total[ACROSS] += overlap(k, across[k])

    single = -total[ACROSS] * level[...]
    weights[...] = (2.0 * single - single.T).astype(weights.dtype)

    @pl.loop(0, CHUNKS)
    def _(k):
        far(k).wait_send()
        pl.when(relays)(lambda: relay(k).wait_send())


def apply_kernel(across, weights, gradient, out, staged, sems):
    width = staged.shape[2]

    def stored(k):
        at = pl.ds(pl.multiple_of(k * width, width), width)
        return pltpu.make_async_copy(staged.at[k], out.at[:, at], sems.at[k])

    @pl.loop(0, CHUNKS)
    def _(k):
        staged[k] = gradient[k] + jnp.dot(
            weights[...], across[k], preferred_element_type=jnp.float32
        )
        stored(k).start()

    @pl.loop(0, CHUNKS)
    def _(k):
        stored(k).wait()


def local(orbital_blocks, eps_occ, eps_vir, pair_mask):
    _, size, aux = orbital_blocks.shape
    width = aux // CHUNKS
    count = lax.axis_size("occ")
    vmem = pl.BlockSpec(memory_space=pltpu.VMEM)
    smem = pl.BlockSpec(memory_space=pltpu.SMEM)
    hbm = pl.BlockSpec(memory_space=pl.ANY)
    per_chunk = pltpu.SemaphoreType.DMA((CHUNKS,))
    arrived = pl.pallas_call(
        functools.partial(gather_kernel, count),
        out_shape=(
            pltpu.VMEM((CHUNKS, size, width), jnp.bfloat16),
            pltpu.VMEM((size, size), jnp.bfloat16),
            pltpu.VMEM((CHUNKS, size, width), jnp.float32),
        ),
        in_specs=[hbm, vmem, smem, smem],
        out_specs=(vmem, vmem, vmem),
        scratch_shapes=[
            pltpu.VMEM((CHUNKS, 2, size, width), jnp.bfloat16),
            pltpu.VMEM((size, 2 * size), jnp.bfloat16),
            pltpu.VMEM((CHUNKS, size, width), jnp.bfloat16),
            pltpu.VMEM((3, size, size), jnp.float32),
            pltpu.VMEM((size, size), jnp.float32),
            per_chunk, per_chunk, per_chunk, per_chunk, per_chunk,
            pltpu.SemaphoreType.DMA((2, CHUNKS)),
            per_chunk,
        ],
        compiler_params=pltpu.CompilerParams(
            collective_id=0, has_side_effects=True, vmem_limit_bytes=44 * 2**20
        ),
    )(orbital_blocks[0], eps_vir[None], eps_occ, pair_mask.T)
    gradient = pl.pallas_call(
        apply_kernel,
        out_shape=jax.ShapeDtypeStruct((size, aux), jnp.float32),
        in_specs=[vmem, vmem, vmem],
        out_specs=hbm,
        scratch_shapes=[
            pltpu.VMEM((CHUNKS, size, width), jnp.float32),
            per_chunk,
        ],
        compiler_params=pltpu.CompilerParams(vmem_limit_bytes=44 * 2**20),
    )(*(pltpu.with_memory_space_constraint(array, pltpu.VMEM) for array in arrived))
    return gradient[None]


def solution(mesh):
    in_specs = (P(("grp", "occ"), None, None), P("grp"), P("grp"), P("grp", None))
    out_specs = P(("grp", "occ"), None, None)
    return jax.shard_map(local, mesh=mesh, in_specs=in_specs, out_specs=out_specs, check_vma=False)
```

```python
import functools

import jax
import jax.numpy as jnp
from jax import lax
from jax.experimental import pallas as pl
from jax.experimental.pallas import tpu as pltpu
from jax.sharding import PartitionSpec as P

MESH = pl.DeviceIdType.MESH
CHUNKS = 8
LOWER, UPPER, ACROSS = 0, 1, 2


def gather_kernel(
    count, own_hbm, eps_vir, eps_occ, mask, across, weights, gradient,
    near, near_weights, own, total, level,
    own_sem, up_sem, down_sem, far_sem, relay_sem, near_recv, across_recv,
):
    me = lax.axis_index("occ")
    half = count // 2
    size, width = own.shape[1:]
    last = count - 1
    partner = lax.rem(me + half, count)
    sends_up = (me < last) & (me != half - 1)
    sends_down = (me > 0) & (me != half)
    relays = (me == 0) | (me == last)
    relayed = (me == half - 1) | (me == half)
    yields = (me == half + 1) | (me == half - 2)
    relay_to = jnp.where(me == 0, half - 1, half)
    relay_slot = jnp.where(me == 0, UPPER, LOWER)
    relay_peer = jnp.where(me == half - 1, 0, jnp.where(me == half, last, relay_to))
    one = lambda flag: jnp.where(flag, 1, 0)

    def signal(to):
        pl.semaphore_signal(
            pltpu.get_barrier_semaphore(), inc=1, device_id={"occ": to}, device_id_type=MESH
        )

    signal(partner)
    pl.when(sends_up)(lambda: signal(me + 1))
    pl.when(sends_down)(lambda: signal(me - 1))
    pl.when(relays | relayed)(lambda: signal(relay_peer))
    pl.semaphore_wait(
        pltpu.get_barrier_semaphore(), 1 + one(sends_up) + one(sends_down) + one(relays | relayed)
    )

    def columns(k):
        return own_hbm.at[:, pl.ds(pl.multiple_of(k * width, width), width)]

    def to_near(source, k, slot, send_sem, to):
        return pltpu.make_async_remote_copy(
            src_ref=source, dst_ref=near.at[k, slot], send_sem=send_sem.at[k],
            recv_sem=near_recv.at[slot, k], device_id={"occ": to}, device_id_type=MESH,
        )

    def up(k):
        return to_near(columns(k), k, LOWER, up_sem, me + 1)

    def down(k):
        return to_near(columns(k), k, UPPER, down_sem, me - 1)

    def relay(k):
        return to_near(across.at[k], k, relay_slot, relay_sem, relay_to)

    def far(k):
        return pltpu.make_async_remote_copy(
            src_ref=columns(k), dst_ref=across.at[k], send_sem=far_sem.at[k],
            recv_sem=across_recv.at[k], device_id={"occ": partner}, device_id_type=MESH,
        )

    def loaded(k):
        return pltpu.make_async_copy(columns(k), own.at[k], own_sem.at[k])

    def send_far(first):
        @pl.loop(first, CHUNKS)
        def _(k):
            far(k).start()

    pl.when(jnp.logical_not(yields))(lambda: far(0).start())

    @pl.loop(0, CHUNKS)
    def _(k):
        pl.when(sends_up)(lambda: up(k).start())
        pl.when(sends_down)(lambda: down(k).start())

    pl.when(jnp.logical_not(yields))(lambda: send_far(1))

    @pl.loop(0, CHUNKS)
    def _(k):
        loaded(k).start()

    rows = jnp.broadcast_to(eps_vir[...], (size, size))
    level[...] = rows + rows.T
    total[...] = jnp.zeros_like(total)

    gradient[...] = jnp.zeros_like(gradient)

    def overlap(k, block):
        return lax.dot_general(
            own[k], block, (((1,), (1,)), ((), ())), preferred_element_type=jnp.float32
        )

    def accumulate(k, slot):
        to_near(near.at[k, slot], k, slot, far_sem, partner).wait_recv()
        total[slot] += overlap(k, near[k, slot])

    def kept(bit):
        return jnp.where(bit == 1, 1.0, 0.0)

    @pl.loop(0, 2)
    def _(turn):
        slot = jnp.where(me == half, 1 - turn, turn)
        other = jnp.where(slot == LOWER, me - 1, me + 1)

        @pl.loop(0, CHUNKS)
        def _(k):
            pl.when(turn == 0)(lambda: loaded(k).wait())
            pl.when((other >= 0) & (other < count))(lambda: accumulate(k, slot))

        @pl.when((other >= 0) & (other < count))
        def _():
            single = -total[slot] / (level[...] - (eps_occ[me] + eps_occ[other]))
            doubled = (2.0 * single - single.T) * kept(mask[0, jnp.minimum(me, other)])
            near_weights[...] = doubled.astype(near_weights.dtype)

            @pl.loop(0, CHUNKS)
            def _(k):
                gradient[k] += jnp.dot(
                    near_weights[...], near[k, slot], preferred_element_type=jnp.float32
                )

    pl.when(yields)(lambda: send_far(0))
    level[...] = kept(mask[1, jnp.minimum(me, partner)]) / (
        level[...] - (eps_occ[me] + eps_occ[partner])
    )

    @pl.loop(0, CHUNKS)
    def _(k):
        pl.when(sends_up)(lambda: up(k).wait_send())
        pl.when(sends_down)(lambda: down(k).wait_send())

    @pl.loop(0, CHUNKS)
    def _(k):
        far(k).wait_recv()
        pl.when(relays)(lambda: relay(k).start())
        total[ACROSS] += overlap(k, across[k])

    single = -total[ACROSS] * level[...]
    weights[...] = (2.0 * single - single.T).astype(weights.dtype)

    @pl.loop(0, CHUNKS)
    def _(k):
        far(k).wait_send()
        pl.when(relays)(lambda: relay(k).wait_send())


def apply_kernel(across, weights, gradient, out, staged, sems):
    width = staged.shape[2]

    def stored(k):
        at = pl.ds(pl.multiple_of(k * width, width), width)
        return pltpu.make_async_copy(staged.at[k], out.at[:, at], sems.at[k])

    @pl.loop(0, CHUNKS)
    def _(k):
        staged[k] = gradient[k] + jnp.dot(
            weights[...], across[k], preferred_element_type=jnp.float32
        )
        stored(k).start()

    @pl.loop(0, CHUNKS)
    def _(k):
        stored(k).wait()


def local(orbital_blocks, eps_occ, eps_vir, pair_mask):
    _, size, aux = orbital_blocks.shape
    width = aux // CHUNKS
    count = lax.axis_size("occ")
    vmem = pl.BlockSpec(memory_space=pltpu.VMEM)
    smem = pl.BlockSpec(memory_space=pltpu.SMEM)
    hbm = pl.BlockSpec(memory_space=pl.ANY)
    per_chunk = pltpu.SemaphoreType.DMA((CHUNKS,))
    arrived = pl.pallas_call(
        functools.partial(gather_kernel, count),
        out_shape=(
            pltpu.VMEM((CHUNKS, size, width), jnp.bfloat16),
            pltpu.VMEM((size, size), jnp.bfloat16),
            pltpu.VMEM((CHUNKS, size, width), jnp.float32),
        ),
        in_specs=[hbm, vmem, smem, smem],
        out_specs=(vmem, vmem, vmem),
        scratch_shapes=[
            pltpu.VMEM((CHUNKS, 2, size, width), jnp.bfloat16),
            pltpu.VMEM((size, size), jnp.bfloat16),
            pltpu.VMEM((CHUNKS, size, width), jnp.bfloat16),
            pltpu.VMEM((3, size, size), jnp.float32),
            pltpu.VMEM((size, size), jnp.float32),
            per_chunk, per_chunk, per_chunk, per_chunk, per_chunk,
            pltpu.SemaphoreType.DMA((2, CHUNKS)),
            per_chunk,
        ],
        compiler_params=pltpu.CompilerParams(
            collective_id=0, has_side_effects=True, vmem_limit_bytes=44 * 2**20
        ),
    )(orbital_blocks[0], eps_vir[None], eps_occ, pair_mask.T)
    gradient = pl.pallas_call(
        apply_kernel,
        out_shape=jax.ShapeDtypeStruct((size, aux), jnp.float32),
        in_specs=[vmem, vmem, vmem],
        out_specs=hbm,
        scratch_shapes=[
            pltpu.VMEM((CHUNKS, size, width), jnp.float32),
            per_chunk,
        ],
        compiler_params=pltpu.CompilerParams(vmem_limit_bytes=44 * 2**20),
    )(*(pltpu.with_memory_space_constraint(array, pltpu.VMEM) for array in arrived))
    return gradient[None]


def solution(mesh):
    in_specs = (P(("grp", "occ"), None, None), P("grp"), P("grp"), P("grp", None))
    out_specs = P(("grp", "occ"), None, None)
    return jax.shard_map(local, mesh=mesh, in_specs=in_specs, out_specs=out_specs, check_vma=False)
```
